256 devices in a mesh: ha: 16 (over y, x), wa: 16 (over z, core).
Axes of the slice: x: 4, y: 4, z: 8, core: 2. Of those that a mesh axis runs over, the one named last changes fastest.
Arguments:
- latent: bfloat16 [720, 640, 96], P('ha', 'wa'), may hold values from -6 to 6
- frame_cache: bfloat16 [2, 720, 640, 96], P(None, 'ha', 'wa'), may hold values from -6 to 6
- norm_gain: float32 [96], replicated, may hold values from 0.5 to 2
- conv_bias: float32 [96], replicated, may hold values from -3 to 3
- conv_weight: bfloat16 [96, 2592], P('ha', 'wa'), may hold values from -0.125 to 0.125
- grad_out: bfloat16 [720, 640, 96], P('ha', 'wa'), may hold values from -6 to 6
Outputs:
- output: bfloat16 [720, 640, 96], P('ha', 'wa')
- grad_latent: bfloat16 [720, 640, 96], P('ha', 'wa')
- grad_weight: float32 [96, 2592], P('ha', 'wa')
The draws below stay inside these ranges and needn't reach their ends.
All inputs are finite; a program needn't handle non-finite values.
Results may differ from the reference program's by a relative error of at most 0.0023.
Values may be sent and summed in bfloat16 or wider, within the bound.
A program may use at most 64 MiB of HBM per device.

```python
import math
import jax
import jax.numpy as jnp
from jax import lax

CHANNELS = 96
TAPS = 3
HEIGHT = 720
WIDTH = 640
KSIZE = 2592


def with_spikes(values, rng, source, target, blocks, factor):
    owner, partner = [(jnp.arange(values.shape[dim]) // (values.shape[dim] // blocks)).reshape([-1 if axis == dim else 1 for axis in range(values.ndim)]) for dim in (source, target)]
    chosen = jax.random.permutation(rng, blocks)[partner]
    strong = (owner == chosen) | (owner == (partner + blocks // 2) % blocks)
    return jnp.where(strong, factor * values, values)


def block_scale(own_key, extent, cuts, smallest, high):
    def one(position, parts):
        heights = jax.random.uniform(jax.random.fold_in(jax.random.fold_in(own_key, 6), position), (parts,), jnp.float32, smallest / len(cuts), high / len(cuts))
        return jnp.repeat(jnp.exp(heights), extent[position] // parts).reshape((-1,) + (1,) * (len(extent) - position - 1))

    gain = one(*cuts[0])
    for cut in cuts[1:]:
        gain = gain * one(*cut)
    return gain


def gaussian(rng, extent, scale, reach, split=(), dtype=jnp.bfloat16):
    entries = jax.random.normal(rng, extent, jnp.float32) * scale
    if len(split) > 0:
        entries = block_scale(rng, extent, split, -0.22, 0.18) * entries
    return jnp.clip(entries, min=-reach, max=reach).astype(dtype)


def heavy_noise(stream_key, shape, scale, most, split, heavy, kind=jnp.bfloat16):
    drawn = scale * jax.random.normal(stream_key, shape, jnp.float32)
    if split:
        drawn = drawn * block_scale(stream_key, shape, split, -0.22, 0.18)
    return jnp.clip(with_spikes(drawn, jax.random.fold_in(stream_key, 3), *heavy), -most, most).astype(kind)


def setup_inputs(seed: int = 0) -> dict:
    streams_of = jax.random.split(jax.random.key(seed), 7)
    latent = gaussian(streams_of[0], (HEIGHT, WIDTH, CHANNELS), 1.0, 6.0, ((0, 16), (1, 16)))
    frame_cache = gaussian(streams_of[1], (TAPS - 1, HEIGHT, WIDTH, CHANNELS), 1.0, 6.0, ((1, 16), (2, 16)))
    norm_gain = jnp.clip(jnp.exp(jax.random.uniform(streams_of[2], (CHANNELS,), jnp.float32, math.log(0.5), math.log(2.0))), 0.5, 2.0)
    conv_bias = gaussian(streams_of[3], (CHANNELS,), 0.5, 3.0, (), jnp.float32)
    conv_weight = gaussian(streams_of[4], (CHANNELS, KSIZE), KSIZE ** -0.5, 0.125, ((0, 16), (1, 16)))
    grad_out = heavy_noise(streams_of[5], (HEIGHT, WIDTH, CHANNELS), 1.0, 6.0, ((0, 16), (1, 16)), (0, 2, 16, 2.0))
    return dict(latent=latent, frame_cache=frame_cache, norm_gain=norm_gain, conv_bias=conv_bias, conv_weight=conv_weight, grad_out=grad_out)


def activate(values, norm_gain):
    scale = lax.rsqrt(lax.optimization_barrier(jnp.mean(values * values, axis=-1, keepdims=True)) + 1e-06)
    return jax.nn.silu(values * scale * norm_gain)

def reference(latent, frame_cache, norm_gain, conv_bias, conv_weight, grad_out):
    channels = latent.shape[2]
    height = latent.shape[0]
    width = latent.shape[1]
    latent_float = latent.astype(jnp.float32)
    activated = activate(latent_float, norm_gain).astype(jnp.bfloat16)
    frames = jnp.concatenate([frame_cache, activated[None]], axis=0)
    padded = jnp.pad(frames, ((0, 0), (1, 1), (1, 1), (0, 0)))
    grad_flat = grad_out.reshape(-1, channels)
    grad_padded = jnp.pad(grad_out, ((1, 1), (1, 1), (0, 0)))
    total = jnp.zeros((height * width, channels), jnp.float32)
    back_total = jnp.zeros((height * width, channels), jnp.float32)
    pieces = []
    for time_tap in range(3):
        for row_tap in range(3):
            for col_tap in range(3):
                offset = (9 * time_tap + 3 * row_tap + col_tap) * channels
                tap_weight = conv_weight[:, offset:offset + channels]
                slab_rows = padded[time_tap, row_tap:row_tap + height, col_tap:col_tap + width].reshape(-1, channels)
                total = total + jnp.dot(slab_rows, tap_weight.T, preferred_element_type=jnp.float32)
                pieces.append(jnp.dot(grad_flat.T, slab_rows, preferred_element_type=jnp.float32))
                if time_tap == 2:
                    shifted = grad_padded[2 - row_tap:2 - row_tap + height, 2 - col_tap:2 - col_tap + width].reshape(-1, channels)
                    back_total = back_total + jnp.dot(shifted, tap_weight, preferred_element_type=jnp.float32)
    output = (latent_float + conv_bias + total.reshape(height, width, channels)).astype(jnp.bfloat16)
    grad_weight = jnp.concatenate(pieces, axis=1)
    unused, pullback = jax.vjp(lambda values: activate(values, norm_gain), latent_float)
    grad_latent = (grad_out.astype(jnp.float32) + pullback(back_total.reshape(height, width, channels))[0]).astype(jnp.bfloat16)
    return (output, grad_latent, grad_weight)
```

```python
import jax
import jax.numpy as jnp
from jax import lax
from jax.experimental import pallas as pl
from jax.experimental.pallas import tpu as pltpu
from jax.sharding import PartitionSpec as P

MESH = pl.DeviceIdType.MESH
F32 = jnp.float32
BF16 = jnp.bfloat16

H = 45
W = 40
C = 96
PITCH = 48
LEAD = 16
FLAT = (H + 2) * PITCH
PIX = H * PITCH
SROWS = LEAD + FLAT + 16
BASE = LEAD + PITCH
KB = 162
HALF = 14 * 128
ROWS = 9
XY = [(dy, dx) for dy in range(4) for dx in range(4) if (dy, dx) != (0, 0)]
XY.sort(key=lambda p: -(min(p[0], 4 - p[0]) + min(p[1], 4 - p[1])))


def slot_of(tap):
    return [tap] if tap < 13 else [13, 14] if tap == 13 else [tap + 1]


def nt(a, b):
    return lax.dot_general(a, b, (((1,), (1,)), ((), ())), preferred_element_type=F32)


def nn(a, b):
    return lax.dot_general(a, b, (((1,), (0,)), ((), ())), preferred_element_type=F32)


def remote(src, dst, send, recv, device):
    return pltpu.make_async_remote_copy(
        src_ref=src, dst_ref=dst, send_sem=send, recv_sem=recv, device_id=device, device_id_type=MESH
    )


def kernel(
    lat_ref, cache_ref, gain_ref, bias_ref, w_ref, gout_ref,
    out_ref, glat_ref, gw_ref,
    S, FS, FG, GT, gpad,
    rowbuf, colsend, colbuf, cornsend, cornbuf,
    Wtmp, Wown, Wp, Wl, Wg, Wn, Wb,
    Rs, RC, SB, RA, T, PZ, RZ,
    row_s, row_r, col_s, col_r, corn_s, corn_r,
    wp_s, wp_r, wg_s, wg_r, wc_s, wc_r,
    rc_s, rc_r, ra_s, ra_r, rz_s, rz_r,
):
    a = lax.axis_index("ha")
    b = lax.axis_index("wa")
    y, x = a // 4, a % 4
    z, core = b // 2, b % 2
    up, down = (a + 15) % 16, (a + 1) % 16
    left, right = (b + 15) % 16, (b + 1) % 16

    barrier = pltpu.get_barrier_semaphore()
    partners = [(a, (b + d) % 16) for d in range(1, 16)]
    partners += [((a + d) % 16, b) for d in range(1, 16)]
    partners += [(v, h) for v in (up, down) for h in (left, right)]
    for p in partners:
        pl.semaphore_signal(barrier, inc=1, device_id=p, device_id_type=MESH)

    S[...] = jnp.zeros_like(S)
    gpad[...] = jnp.zeros_like(gpad)
    gpad[:, 0:C] = gain_ref[...]
    Wtmp[...] = jnp.zeros_like(Wtmp)
    Wtmp[0:6, 0:KB] = w_ref[...].astype(F32)
    Wown[...] = Wtmp[...].astype(BF16)

    @pl.loop(0, H)
    def _(h):
        row = pl.multiple_of(BASE + h * PITCH, 8)
        S[0, pl.ds(row, W), 0:C] = cache_ref[0, h].astype(F32)
        S[1, pl.ds(row, W), 0:C] = cache_ref[1, h].astype(F32)
        S[2, pl.ds(row, W), 0:C] = lat_ref[h].astype(F32)
        S[3, pl.ds(row, W), 0:C] = gout_ref[h].astype(F32)

    for n in range(4):
        colsend[0, n, 0:H] = S[n, pl.ds(BASE, H, stride=PITCH)].astype(BF16)
        colsend[1, n, 0:H] = S[n, pl.ds(BASE + W - 1, H, stride=PITCH)].astype(BF16)
        for k, (r, c) in enumerate(((0, 0), (0, W - 1), (H - 1, 0), (H - 1, W - 1))):
            at = BASE + r * PITCH + c
            cornsend[k, n : n + 1] = S[n, at : at + 1]

    pl.semaphore_wait(barrier, len(partners))

    halo = []
    for k, (r, dev) in enumerate(((H - 1, (down, b)), (0, (up, b)))):
        for m, (src, dst) in enumerate(
            (
                (cache_ref.at[:, r], rowbuf.at[k, pl.ds(0, 2)]),
                (lat_ref.at[r], rowbuf.at[k, 2]),
                (gout_ref.at[r], rowbuf.at[k, 3]),
            )
        ):
            halo.append(remote(src, dst, row_s.at[k, m], row_r.at[k, m], dev))
    for k, dev in enumerate(((a, left), (a, right))):
        halo.append(remote(colsend.at[k], colbuf.at[k], col_s.at[k], col_r.at[k], dev))
    for k, dev in enumerate(((up, left), (up, right), (down, left), (down, right))):
        halo.append(remote(cornsend.at[k], cornbuf.at[k], corn_s.at[k], corn_r.at[k], dev))
    for copy in halo:
        copy.start()
    wpieces = [
        remote(Wown, Wp.at[b], wp_s.at[d - 1], wp_r.at[d - 1], (a, (b + d) % 16))
        for d in range(1, 16)
    ]
    for copy in wpieces:
        copy.start()
    Wp[b] = Wown[...]

    row_id = lax.broadcasted_iota(jnp.int32, (128, 128), 0)
    col_id = lax.broadcasted_iota(jnp.int32, (128, 128), 1)
    spread = (row_id % 8 < 6) & (col_id == (row_id // 8) * 6 + row_id % 8)
    spread = jnp.where(spread, 1.0, 0.0).astype(BF16)
    GT[...] = nt(spread, S[3, BASE : BASE + PIX].astype(BF16)).astype(BF16)

    for copy in halo:
        copy.wait_recv()
    for n in range(4):
        S[n, LEAD : LEAD + W, 0:C] = jnp.where(a > 0, rowbuf[0, n].astype(F32), 0.0)
        S[n, BASE + PIX : BASE + PIX + W, 0:C] = jnp.where(a < 15, rowbuf[1, n].astype(F32), 0.0)
        S[n, pl.ds(BASE + W, H, stride=PITCH)] = jnp.where(
            b < 15, colbuf[0, n, 0:H].astype(F32), 0.0
        )
        S[n, pl.ds(BASE - 1, H, stride=PITCH)] = jnp.where(
            b > 0, colbuf[1, n, 0:H].astype(F32), 0.0
        )
        for k, (at, there) in enumerate(
            (
                (BASE + PIX + W, (a < 15) & (b < 15)),
                (BASE + PIX - 1, (a < 15) & (b > 0)),
                (LEAD + W, (a > 0) & (b < 15)),
                (LEAD - 1, (a > 0) & (b > 0)),
            )
        ):
            S[n, at : at + 1] = jnp.where(there, cornbuf[k, n : n + 1], 0.0)

    gain = gpad[...]

    @pl.loop(0, SROWS // 176)
    def _(i):
        rows = pl.ds(pl.multiple_of(i * 176, 8), 176)
        v = S[2, rows]
        scale = lax.rsqrt(jnp.sum(v * v, axis=1, keepdims=True) * (1.0 / C) + 1e-06)
        n = v * scale * gain
        S[2, rows] = n / (1.0 + jnp.exp(-n))

    @pl.loop(0, 3)
    def _(i):
        at = pl.multiple_of(i * 752, 16)
        for n in range(4):
            block = S[n, pl.ds(at, 784)]
            for c in range(3):
                part = block[15 + c : 15 + c + 752].astype(BF16)
                k = 3 * c + n
                if n < 3:
                    FS[pl.ds(at, 752), k * 128 : (k + 1) * 128] = part
                else:
                    FG[pl.ds(at, 752), c * 128 : (c + 1) * 128] = part

    for copy in wpieces:
        copy.wait_recv()
    lane = lax.broadcasted_iota(jnp.int32, (8, 256), 1)
    for tap in range(27):
        total = jnp.zeros((8, 256), F32)
        for j in range(16):
            shift = KB * j - C * tap
            lo, hi = max(0, shift), min(C, shift + KB)
            if lo < hi:
                moved = pltpu.roll(Wp[j].astype(F32), shift % 256, 1)
                total += jnp.where((lane >= lo) & (lane < hi), moved, 0.0)
        for s in slot_of(tap):
            Wl[:, s * 128 : (s + 1) * 128] = total[:, 0:128].astype(BF16)
    mine = pl.ds(pl.multiple_of(core * HALF, 128), HALF)
    other = pl.ds(pl.multiple_of((1 - core) * HALF, 128), HALF)
    peers = [((y + dy) % 4 * 4 + (x + dx) % 4, b) for dy, dx in XY]
    partner = (a, z * 2 + 1 - core)
    wsends = [
        remote(Wl.at[:, mine], Wg.at[a, :, mine], wg_s.at[k], wg_r.at[k], p)
        for k, p in enumerate(peers)
    ]
    for copy in wsends:
        copy.start()
    Wg[a, :, mine] = Wl[:, mine]

    for r in range(3):
        part = nn(GT[...], FS[PITCH * r : PITCH * r + PIX])
        for c in range(3):
            for t in range(3):
                k = 3 * c + t
                block = part[:, k * 128 : (k + 1) * 128].reshape(16, 8, 128)
                for s in slot_of(9 * t + 3 * r + c):
                    Rs[:, :, s * 128 : (s + 1) * 128] = block
    pair = remote(Rs.at[:, :, other], RC, rc_s, rc_r, partner)
    pair.start()

    for copy in wsends:
        copy.wait_recv()
    wswap = remote(Wg.at[:, :, mine], Wg.at[:, :, mine], wc_s, wc_r, partner)
    wswap.start()

    pair.wait_recv()

    @pl.loop(0, 16)
    def _(k):
        SB[k] = (Rs[k, :, mine] + RC[k]).astype(SB.dtype)

    asends = [
        remote(SB.at[p[0]], RA.at[k], ra_s.at[k], ra_r.at[k], p) for k, p in enumerate(peers)
    ]
    for copy in asends:
        copy.start()

    wswap.wait()
    compact = (row_id < C) & (col_id == (row_id // 6) * 8 + row_id % 6)
    compact = jnp.where(compact, 1.0, 0.0).astype(BF16)
    for tap in range(27):
        s = slot_of(tap)[0]
        block = Wg[:, :, s * 128 : (s + 1) * 128].astype(F32).reshape(128, 128)
        block = nn(compact, block.astype(BF16)).astype(BF16)
        t, r, c = tap // 9, tap // 3 % 3, tap % 3
        Wn[r, :, (3 * c + t) * 128 : (3 * c + t + 1) * 128] = block
        if t == 2:
            Wb[r, (2 - c) * 128 : (3 - c) * 128] = block

    @pl.loop(0, H // ROWS)
    def _(i):
        h0 = i * ROWS
        at = pl.multiple_of(h0 * PITCH, 16)
        acc = nt(FS[pl.ds(at, ROWS * PITCH)], Wn[0])
        acc += nt(FS[pl.ds(at + PITCH, ROWS * PITCH)], Wn[1])
        acc += nt(FS[pl.ds(at + 2 * PITCH, ROWS * PITCH)], Wn[2])
        acc = acc.reshape(ROWS, PITCH, 128)[:, 0:W, 0:C]
        lat = lat_ref[pl.ds(h0, ROWS)].astype(F32)
        out_ref[pl.ds(h0, ROWS)] = (lat + bias_ref[...].reshape(1, 1, C) + acc).astype(BF16)

        back = nn(FG[pl.ds(at + 2 * PITCH, ROWS * PITCH)], Wb[0])
        back += nn(FG[pl.ds(at + PITCH, ROWS * PITCH)], Wb[1])
        back += nn(FG[pl.ds(at, ROWS * PITCH)], Wb[2])
        dact = back.reshape(ROWS, PITCH, 128)[:, 0:W, 0:C]
        g = gain_ref[...].reshape(1, 1, C)
        scale = lax.rsqrt(jnp.sum(lat * lat, axis=2, keepdims=True) * (1.0 / C) + 1e-06)
        n = lat * scale * g
        sig = 1.0 / (1.0 + jnp.exp(-n))
        du = dact * (sig * (1.0 + n * (1.0 - sig))) * g
        inner = jnp.sum(lat * du, axis=2, keepdims=True) * (1.0 / C)
        dlat = scale * du - lat * (scale * scale * scale * inner)
        glat_ref[pl.ds(h0, ROWS)] = (gout_ref[pl.ds(h0, ROWS)].astype(F32) + dlat).astype(BF16)

    total = Rs[a, :, mine] + RC[a]
    for k, copy in enumerate(asends):
        copy.wait_recv()
        total += RA[k].astype(F32)
    T[...] = total
    for half in range(2):

        @pl.when(core == half)
        def _():
            for j in range(8):
                piece = jnp.zeros((8, 256), F32)
                for m in range(14):
                    shift = C * m - (KB * j + 48 * half)
                    lo, hi = max(0, shift), min(KB, shift + C)
                    if lo < hi:
                        block = jnp.concatenate(
                            [T[:, m * 128 : (m + 1) * 128], jnp.zeros((8, 128), F32)], axis=1
                        )
                        moved = pltpu.roll(block, shift % 256, 1)
                        piece += jnp.where((lane >= lo) & (lane < hi), moved, 0.0)
                PZ[j] = piece

    zsends = []
    for j in range(8):
        oz, oc = 4 * core + j // 2, j % 2
        itself = (oz == z) & (oc == core)
        copy = remote(PZ.at[j], RZ.at[z], rz_s.at[j], rz_r.at[z], (a, oz * 2 + oc))
        zsends.append((itself, copy))

        @pl.when(jnp.logical_not(itself))
        def _():
            copy.start()

        @pl.when(itself)
        def _():
            RZ[z] = PZ[j]

    for k in range(8):
        source = (a, k * 2 + z // 4)

        @pl.when(jnp.logical_not((k == z) & (z // 4 == core)))
        def _():
            remote(PZ.at[0], RZ.at[k], rz_s.at[0], rz_r.at[k], source).wait_recv()

    final = RZ[0]
    for k in range(1, 8):
        final += RZ[k]
    gw_ref[...] = final[0:6, 0:KB]

    for copy in halo + wpieces + wsends + asends:
        copy.wait_send()
    pair.wait_send()
    for itself, copy in zsends:

        @pl.when(jnp.logical_not(itself))
        def _():
            copy.wait_send()


def local(latent, frame_cache, norm_gain, conv_bias, conv_weight, grad_out):
    vmem = pl.BlockSpec(memory_space=pltpu.VMEM)
    dma = pltpu.SemaphoreType.DMA
    return pl.pallas_call(
        kernel,
        out_shape=(
            jax.ShapeDtypeStruct((H, W, C), BF16),
            jax.ShapeDtypeStruct((H, W, C), BF16),
            jax.ShapeDtypeStruct((6, KB), F32),
        ),
        in_specs=[vmem] * 6,
        out_specs=(vmem, vmem, vmem),
        scratch_shapes=[
            pltpu.VMEM((4, SROWS, 128), F32),
            pltpu.VMEM((FLAT, 9 * 128), BF16),
            pltpu.VMEM((FLAT, 3 * 128), BF16),
            pltpu.VMEM((128, PIX), BF16),
            pltpu.VMEM((1, 128), F32),
            pltpu.VMEM((2, 4, W, C), BF16),
            pltpu.VMEM((2, 4, 48, 128), BF16),
            pltpu.VMEM((2, 4, 48, 128), BF16),
            pltpu.VMEM((4, 8, 128), F32),
            pltpu.VMEM((4, 8, 128), F32),
            pltpu.VMEM((8, 256), F32),
            pltpu.VMEM((8, 256), BF16),
            pltpu.VMEM((16, 8, 256), BF16),
            pltpu.VMEM((8, 2 * HALF), BF16),
            pltpu.VMEM((16, 8, 2 * HALF), BF16),
            pltpu.VMEM((3, 128, 9 * 128), BF16),
            pltpu.VMEM((3, 3 * 128, 128), BF16),
            pltpu.VMEM((16, 8, 2 * HALF), F32),
            pltpu.VMEM((16, 8, HALF), F32),
            pltpu.VMEM((16, 8, HALF), F32),
            pltpu.VMEM((15, 8, HALF), F32),
            pltpu.VMEM((8, HALF), F32),
            pltpu.VMEM((8, 8, 256), F32),
            pltpu.VMEM((8, 8, 256), F32),
            dma((2, 3)), dma((2, 3)), dma((2,)), dma((2,)), dma((4,)), dma((4,)),
            dma((15,)), dma((15,)), dma((15,)), dma((15,)), dma, dma,
            dma, dma, dma((15,)), dma((15,)), dma((8,)), dma((8,)),
        ],
        compiler_params=pltpu.CompilerParams(
            collective_id=0, has_side_effects=True, vmem_limit_bytes=60 * 1024 * 1024
        ),
    )(
        latent, frame_cache, norm_gain.reshape(1, C), conv_bias.reshape(1, C), conv_weight, grad_out
    )


def solution(mesh):
    placed = (
        P("ha", "wa", None),
        P(None, "ha", "wa", None),
        P(),
        P(),
        P("ha", "wa"),
        P("ha", "wa", None),
    )
    return jax.shard_map(
        local,
        mesh=mesh,
        in_specs=placed,
        out_specs=(P("ha", "wa", None), P("ha", "wa", None), P("ha", "wa")),
        check_vma=False,
    )
```

```python
import jax
import jax.numpy as jnp
from jax import lax
from jax.experimental import pallas as pl
from jax.experimental.pallas import tpu as pltpu
from jax.sharding import PartitionSpec as P

MESH = pl.DeviceIdType.MESH
F32 = jnp.float32
BF16 = jnp.bfloat16

H = 45
W = 40
C = 96
PITCH = 48
LEAD = 16
FLAT = (H + 2) * PITCH
PIX = H * PITCH
SROWS = LEAD + FLAT + 16
BASE = LEAD + PITCH
KB = 162
HALF = 14 * 128
ROWS = 9
EARLY = 3
XY = [(dy, dx) for dy in range(4) for dx in range(4) if (dy, dx) != (0, 0)]
XY.sort(key=lambda p: -(min(p[0], 4 - p[0]) + min(p[1], 4 - p[1])))


def slot_of(tap):
    return [tap] if tap < 13 else [13, 14] if tap == 13 else [tap + 1]


def nt(a, b):
    return lax.dot_general(a, b, (((1,), (1,)), ((), ())), preferred_element_type=F32)


def nn(a, b):
    return lax.dot_general(a, b, (((1,), (0,)), ((), ())), preferred_element_type=F32)


def remote(src, dst, send, recv, device):
    return pltpu.make_async_remote_copy(
        src_ref=src, dst_ref=dst, send_sem=send, recv_sem=recv, device_id=device, device_id_type=MESH
    )


def kernel(
    lat_ref, cache_ref, gain_ref, bias_ref, w_ref, gout_ref,
    out_ref, glat_ref, gw_ref,
    S, FS, FG, GT, gpad,
    rowbuf, colsend, colbuf, cornsend, cornbuf,
    Wtmp, Wown, Wp, Wl, Wg, Wn, Wb,
    Rs, RP, RC, SB, RA, T, PZ, RZ,
    row_s, row_r, col_s, col_r, corn_s, corn_r,
    wp_s, wp_r, wg_s, wg_r, wc_s, wc_r,
    rc_s, rc_r, ra_s, ra_r, rz_s, rz_r,
):
    a = lax.axis_index("ha")
    b = lax.axis_index("wa")
    y, x = a // 4, a % 4
    z, core = b // 2, b % 2
    up, down = (a + 15) % 16, (a + 1) % 16
    left, right = (b + 15) % 16, (b + 1) % 16

    barrier = pltpu.get_barrier_semaphore()
    partners = [(a, (b + d) % 16) for d in range(1, 16)]
    partners += [((a + d) % 16, b) for d in range(1, 16)]
    partners += [(v, h) for v in (up, down) for h in (left, right)]
    for p in partners:
        pl.semaphore_signal(barrier, inc=1, device_id=p, device_id_type=MESH)

    S[...] = jnp.zeros_like(S)
    gpad[...] = jnp.zeros_like(gpad)
    gpad[:, 0:C] = gain_ref[...]
    Wtmp[...] = jnp.zeros_like(Wtmp)
    Wtmp[0:6, 0:KB] = w_ref[...].astype(F32)
    Wown[...] = Wtmp[...].astype(BF16)

    @pl.loop(0, H)
    def _(h):
        row = pl.multiple_of(BASE + h * PITCH, 8)
        S[0, pl.ds(row, W), 0:C] = cache_ref[0, h].astype(F32)
        S[1, pl.ds(row, W), 0:C] = cache_ref[1, h].astype(F32)
        S[2, pl.ds(row, W), 0:C] = lat_ref[h].astype(F32)
        S[3, pl.ds(row, W), 0:C] = gout_ref[h].astype(F32)

    for n in range(4):
        colsend[0, n, 0:H] = S[n, pl.ds(BASE, H, stride=PITCH)].astype(BF16)
        colsend[1, n, 0:H] = S[n, pl.ds(BASE + W - 1, H, stride=PITCH)].astype(BF16)
        for k, (r, c) in enumerate(((0, 0), (0, W - 1), (H - 1, 0), (H - 1, W - 1))):
            at = BASE + r * PITCH + c
            cornsend[k, n : n + 1] = S[n, at : at + 1]

    pl.semaphore_wait(barrier, len(partners))

    halo = []
    for k, (r, dev) in enumerate(((H - 1, (down, b)), (0, (up, b)))):
        for m, (src, dst) in enumerate(
            (
                (cache_ref.at[:, r], rowbuf.at[k, pl.ds(0, 2)]),
                (lat_ref.at[r], rowbuf.at[k, 2]),
                (gout_ref.at[r], rowbuf.at[k, 3]),
            )
        ):
            halo.append(remote(src, dst, row_s.at[k, m], row_r.at[k, m], dev))
    for k, dev in enumerate(((a, left), (a, right))):
        halo.append(remote(colsend.at[k], colbuf.at[k], col_s.at[k], col_r.at[k], dev))
    for k, dev in enumerate(((up, left), (up, right), (down, left), (down, right))):
        halo.append(remote(cornsend.at[k], cornbuf.at[k], corn_s.at[k], corn_r.at[k], dev))
    for copy in halo:
        copy.start()
    wpieces = [
        remote(Wown, Wp.at[b], wp_s.at[d - 1], wp_r.at[d - 1], (a, (b + d) % 16))
        for d in range(1, 16)
    ]
    for copy in wpieces:
        copy.start()
    Wp[b] = Wown[...]

    row_id = lax.broadcasted_iota(jnp.int32, (128, 128), 0)
    col_id = lax.broadcasted_iota(jnp.int32, (128, 128), 1)
    spread = (row_id % 8 < 6) & (col_id == (row_id // 8) * 6 + row_id % 8)
    spread = jnp.where(spread, 1.0, 0.0).astype(BF16)
    GT[...] = nt(spread, S[3, BASE : BASE + PIX].astype(BF16)).astype(BF16)

    for copy in wpieces:
        copy.wait_recv()
    lane = lax.broadcasted_iota(jnp.int32, (8, 256), 1)
    for tap in range(27):
        total = jnp.zeros((8, 256), F32)
        for j in range(16):
            shift = KB * j - C * tap
            lo, hi = max(0, shift), min(C, shift + KB)
            if lo < hi:
                moved = pltpu.roll(Wp[j].astype(F32), shift % 256, 1)
                total += jnp.where((lane >= lo) & (lane < hi), moved, 0.0)
        for s in slot_of(tap):
            Wl[:, s * 128 : (s + 1) * 128] = total[:, 0:128].astype(BF16)
    mine = pl.ds(pl.multiple_of(core * HALF, 128), HALF)
    other = pl.ds(pl.multiple_of((1 - core) * HALF, 128), HALF)
    peers = [((y + dy) % 4 * 4 + (x + dx) % 4, b) for dy, dx in XY]
    partner = (a, z * 2 + 1 - core)
    wsends = [
        remote(Wl.at[:, mine], Wg.at[a, :, mine], wg_s.at[k], wg_r.at[k], p)
        for k, p in enumerate(peers)
    ]
    for copy in wsends:
        copy.start()
    Wg[a, :, mine] = Wl[:, mine]

    for copy in halo:
        copy.wait_recv()
    for n in range(4):
        S[n, LEAD : LEAD + W, 0:C] = jnp.where(a > 0, rowbuf[0, n].astype(F32), 0.0)
        S[n, BASE + PIX : BASE + PIX + W, 0:C] = jnp.where(a < 15, rowbuf[1, n].astype(F32), 0.0)
        S[n, pl.ds(BASE + W, H, stride=PITCH)] = jnp.where(
            b < 15, colbuf[0, n, 0:H].astype(F32), 0.0
        )
        S[n, pl.ds(BASE - 1, H, stride=PITCH)] = jnp.where(
            b > 0, colbuf[1, n, 0:H].astype(F32), 0.0
        )
        for k, (at, there) in enumerate(
            (
                (BASE + PIX + W, (a < 15) & (b < 15)),
                (BASE + PIX - 1, (a < 15) & (b > 0)),
                (LEAD + W, (a > 0) & (b < 15)),
                (LEAD - 1, (a > 0) & (b > 0)),
            )
        ):
            S[n, at : at + 1] = jnp.where(there, cornbuf[k, n : n + 1], 0.0)

    gain = gpad[...]

    @pl.loop(0, SROWS // 176)
    def _(i):
        rows = pl.ds(pl.multiple_of(i * 176, 8), 176)
        v = S[2, rows]
        scale = lax.rsqrt(jnp.sum(v * v, axis=1, keepdims=True) * (1.0 / C) + 1e-06)
        n = v * scale * gain
        S[2, rows] = n / (1.0 + jnp.exp(-n))

    @pl.loop(0, 3)
    def _(i):
        at = pl.multiple_of(i * 752, 16)
        for n in range(3):
            block = S[n, pl.ds(at, 784)]
            for c in range(3):
                k = 3 * c + n
                FS[pl.ds(at, 752), k * 128 : (k + 1) * 128] = block[15 + c : 15 + c + 752].astype(
                    BF16
                )

    for r in range(3):
        part = nn(GT[...], FS[PITCH * r : PITCH * r + PIX])
        for c in range(3):
            for t in range(3):
                k = 3 * c + t
                block = part[:, k * 128 : (k + 1) * 128].reshape(16, 8, 128)
                for s in slot_of(9 * t + 3 * r + c):
                    Rs[:, :, s * 128 : (s + 1) * 128] = block
        if r == 1:
            for copy in wsends:
                copy.wait_recv()
            wswap = remote(Wg.at[:, :, mine], Wg.at[:, :, mine], wc_s, wc_r, partner)
            wswap.start()

    @pl.loop(0, 16)
    def _(k):
        RP[k] = Rs[k, :, other].astype(BF16)

    pair = remote(RP, RC, rc_s, rc_r, partner)
    pair.start()

    @pl.loop(0, 3)
    def _(i):
        at = pl.multiple_of(i * 752, 16)
        block = S[3, pl.ds(at, 784)]
        for c in range(3):
            FG[pl.ds(at, 752), c * 128 : (c + 1) * 128] = block[15 + c : 15 + c + 752].astype(BF16)

    pair.wait_recv()

    @pl.loop(0, 16)
    def _(k):
        SB[k] = (Rs[k, :, mine] + RC[k].astype(F32)).astype(BF16)

    asends = [
        remote(SB.at[p[0]], RA.at[k], ra_s.at[k], ra_r.at[k], p) for k, p in enumerate(peers)
    ]
    for copy in asends:
        copy.start()

    wswap.wait()
    compact = (row_id < C) & (col_id == (row_id // 6) * 8 + row_id % 6)
    compact = jnp.where(compact, 1.0, 0.0).astype(BF16)
    for tap in range(27):
        s = slot_of(tap)[0]
        block = Wg[:, :, s * 128 : (s + 1) * 128].astype(F32).reshape(128, 128)
        block = nn(compact, block.astype(BF16)).astype(BF16)
        t, r, c = tap // 9, tap // 3 % 3, tap % 3
        Wn[r, :, (3 * c + t) * 128 : (3 * c + t + 1) * 128] = block
        if t == 2:
            Wb[r, (2 - c) * 128 : (3 - c) * 128] = block

    def rows_step(i):
        h0 = i * ROWS
        at = pl.multiple_of(h0 * PITCH, 16)
        acc = nt(FS[pl.ds(at, ROWS * PITCH)], Wn[0])
        acc += nt(FS[pl.ds(at + PITCH, ROWS * PITCH)], Wn[1])
        acc += nt(FS[pl.ds(at + 2 * PITCH, ROWS * PITCH)], Wn[2])
        acc = acc.reshape(ROWS, PITCH, 128)[:, 0:W, 0:C]
        lat = lat_ref[pl.ds(h0, ROWS)].astype(F32)
        out_ref[pl.ds(h0, ROWS)] = (lat + bias_ref[...].reshape(1, 1, C) + acc).astype(BF16)

        back = nn(FG[pl.ds(at + 2 * PITCH, ROWS * PITCH)], Wb[0])
        back += nn(FG[pl.ds(at + PITCH, ROWS * PITCH)], Wb[1])
        back += nn(FG[pl.ds(at, ROWS * PITCH)], Wb[2])
        dact = back.reshape(ROWS, PITCH, 128)[:, 0:W, 0:C]
        g = gain_ref[...].reshape(1, 1, C)
        scale = lax.rsqrt(jnp.sum(lat * lat, axis=2, keepdims=True) * (1.0 / C) + 1e-06)
        n = lat * scale * g
        sig = 1.0 / (1.0 + jnp.exp(-n))
        du = dact * (sig * (1.0 + n * (1.0 - sig))) * g
        inner = jnp.sum(lat * du, axis=2, keepdims=True) * (1.0 / C)
        dlat = scale * du - lat * (scale * scale * scale * inner)
        glat_ref[pl.ds(h0, ROWS)] = (gout_ref[pl.ds(h0, ROWS)].astype(F32) + dlat).astype(BF16)

    pl.loop(0, EARLY)(rows_step)

    total = Rs[a, :, mine] + RC[a].astype(F32)
    for k, copy in enumerate(asends):
        copy.wait_recv()
        total += RA[k].astype(F32)
    T[...] = total
    for half in range(2):

        @pl.when(core == half)
        def _():
            for j in range(8):
                piece = jnp.zeros((8, 256), F32)
                for m in range(14):
                    shift = C * m - (KB * j + 48 * half)
                    lo, hi = max(0, shift), min(KB, shift + C)
                    if lo < hi:
                        block = jnp.concatenate(
                            [T[:, m * 128 : (m + 1) * 128], jnp.zeros((8, 128), F32)], axis=1
                        )
                        moved = pltpu.roll(block, shift % 256, 1)
                        piece += jnp.where((lane >= lo) & (lane < hi), moved, 0.0)
                PZ[j] = piece

    zsends = []
    for j in range(8):
        oz, oc = 4 * core + j // 2, j % 2
        itself = (oz == z) & (oc == core)
        copy = remote(PZ.at[j], RZ.at[z], rz_s.at[j], rz_r.at[z], (a, oz * 2 + oc))
        zsends.append((itself, copy))

        @pl.when(jnp.logical_not(itself))
        def _():
            copy.start()

        @pl.when(itself)
        def _():
            RZ[z] = PZ[j]

    pl.loop(EARLY, H // ROWS)(rows_step)

    for k in range(8):
        source = (a, k * 2 + z // 4)

        @pl.when(jnp.logical_not((k == z) & (z // 4 == core)))
        def _():
            remote(PZ.at[0], RZ.at[k], rz_s.at[0], rz_r.at[k], source).wait_recv()

    final = RZ[0]
    for k in range(1, 8):
        final += RZ[k]
    gw_ref[...] = final[0:6, 0:KB]

    for copy in halo + wpieces + wsends + asends:
        copy.wait_send()
    pair.wait_send()
    for itself, copy in zsends:

        @pl.when(jnp.logical_not(itself))
        def _():
            copy.wait_send()


def local(latent, frame_cache, norm_gain, conv_bias, conv_weight, grad_out):
    vmem = pl.BlockSpec(memory_space=pltpu.VMEM)
    dma = pltpu.SemaphoreType.DMA
    return pl.pallas_call(
        kernel,
        out_shape=(
            jax.ShapeDtypeStruct((H, W, C), BF16),
            jax.ShapeDtypeStruct((H, W, C), BF16),
            jax.ShapeDtypeStruct((6, KB), F32),
        ),
        in_specs=[vmem] * 6,
        out_specs=(vmem, vmem, vmem),
        scratch_shapes=[
            pltpu.VMEM((4, SROWS, 128), F32),
            pltpu.VMEM((FLAT, 9 * 128), BF16),
            pltpu.VMEM((FLAT, 3 * 128), BF16),
            pltpu.VMEM((128, PIX), BF16),
            pltpu.VMEM((1, 128), F32),
            pltpu.VMEM((2, 4, W, C), BF16),
            pltpu.VMEM((2, 4, 48, 128), BF16),
            pltpu.VMEM((2, 4, 48, 128), BF16),
            pltpu.VMEM((4, 8, 128), F32),
            pltpu.VMEM((4, 8, 128), F32),
            pltpu.VMEM((8, 256), F32),
            pltpu.VMEM((8, 256), BF16),
            pltpu.VMEM((16, 8, 256), BF16),
            pltpu.VMEM((8, 2 * HALF), BF16),
            pltpu.VMEM((16, 8, 2 * HALF), BF16),
            pltpu.VMEM((3, 128, 9 * 128), BF16),
            pltpu.VMEM((3, 3 * 128, 128), BF16),
            pltpu.VMEM((16, 8, 2 * HALF), F32),
            pltpu.VMEM((16, 8, HALF), BF16),
            pltpu.VMEM((16, 8, HALF), BF16),
            pltpu.VMEM((16, 8, HALF), BF16),
            pltpu.VMEM((15, 8, HALF), BF16),
            pltpu.VMEM((8, HALF), F32),
            pltpu.VMEM((8, 8, 256), F32),
            pltpu.VMEM((8, 8, 256), F32),
            dma((2, 3)), dma((2, 3)), dma((2,)), dma((2,)), dma((4,)), dma((4,)),
            dma((15,)), dma((15,)), dma((15,)), dma((15,)), dma, dma,
            dma, dma, dma((15,)), dma((15,)), dma((8,)), dma((8,)),
        ],
        compiler_params=pltpu.CompilerParams(
            collective_id=0, has_side_effects=True, vmem_limit_bytes=60 * 1024 * 1024
        ),
    )(
        latent, frame_cache, norm_gain.reshape(1, C), conv_bias.reshape(1, C), conv_weight, grad_out
    )


def solution(mesh):
    placed = (
        P("ha", "wa", None),
        P(None, "ha", "wa", None),
        P(),
        P(),
        P("ha", "wa"),
        P("ha", "wa", None),
    )
    return jax.shard_map(
        local,
        mesh=mesh,
        in_specs=placed,
        out_specs=(P("ha", "wa", None), P("ha", "wa", None), P("ha", "wa")),
        check_vma=False,
    )
```

```python
import jax
import jax.numpy as jnp
from jax import lax
from jax.experimental import pallas as pl
from jax.experimental.pallas import tpu as pltpu
from jax.sharding import PartitionSpec as P

MESH = pl.DeviceIdType.MESH
F32 = jnp.float32
BF16 = jnp.bfloat16

H = 45
W = 40
C = 96
PITCH = 48
LEAD = 16
FLAT = (H + 2) * PITCH
PIX = H * PITCH
SROWS = LEAD + FLAT + 16
BASE = LEAD + PITCH
KB = 162
HALF = 14 * 128
ROWS = 9
EARLY = 3
XY = [(dy, dx) for dy in range(4) for dx in range(4) if (dy, dx) != (0, 0)]
XY.sort(key=lambda p: -(min(p[0], 4 - p[0]) + min(p[1], 4 - p[1])))


ORDER = (
    (0, 1, 2, 9, 10, 11, 3, 4, 5, 12, 13, 6, 7, 8),
    (18, 19, 20, 13, 14, 21, 22, 23, 15, 16, 17, 24, 25, 26),
)
CHUNKS = ((0, 3), (3, 8), (8, 14))
SUMS = ((0, 8), (8, 14))


def slot_of(tap):
    return [14 * half + ORDER[half].index(tap) for half in (0, 1) if tap in ORDER[half]]


def tiles(core, lo, hi):
    return pl.ds(pl.multiple_of(core * HALF + lo * 128, 128), (hi - lo) * 128)


def nt(a, b):
    return lax.dot_general(a, b, (((1,), (1,)), ((), ())), preferred_element_type=F32)


def nn(a, b):
    return lax.dot_general(a, b, (((1,), (0,)), ((), ())), preferred_element_type=F32)


def remote(src, dst, send, recv, device):
    return pltpu.make_async_remote_copy(
        src_ref=src, dst_ref=dst, send_sem=send, recv_sem=recv, device_id=device, device_id_type=MESH
    )


def kernel(
    lat_ref, cache_ref, gain_ref, bias_ref, w_ref, gout_ref,
    out_ref, glat_ref, gw_ref,
    S, FS, FG, GT, gpad,
    rowbuf, colsend, colbuf, cornsend, cornbuf,
    Wtmp, Wown, Wp, Wl, Wg, Wn, Wb,
    Rs, RC, SB, RA, T, PZ, RZ,
    row_s, row_r, col_s, col_r, corn_s, corn_r,
    wp_s, wp_r, wg_s, wg_r, wc_s, wc_r,
    rc_s, rc_r, ra_s, ra_r, rz_s, rz_r,
):
    a = lax.axis_index("ha")
    b = lax.axis_index("wa")
    y, x = a // 4, a % 4
    z, core = b // 2, b % 2
    up, down = (a + 15) % 16, (a + 1) % 16
    left, right = (b + 15) % 16, (b + 1) % 16

    barrier = pltpu.get_barrier_semaphore()
    partners = [(a, (b + d) % 16) for d in range(1, 16)]
    partners += [((a + d) % 16, b) for d in range(1, 16)]
    partners += [(v, h) for v in (up, down) for h in (left, right)]
    for p in partners:
        pl.semaphore_signal(barrier, inc=1, device_id=p, device_id_type=MESH)

    S[...] = jnp.zeros_like(S)
    gpad[...] = jnp.zeros_like(gpad)
    gpad[:, 0:C] = gain_ref[...]
    Wtmp[...] = jnp.zeros_like(Wtmp)
    Wtmp[0:6, 0:KB] = w_ref[...].astype(F32)
    Wown[...] = Wtmp[...].astype(BF16)

    @pl.loop(0, H)
    def _(h):
        row = pl.multiple_of(BASE + h * PITCH, 8)
        S[0, pl.ds(row, W), 0:C] = cache_ref[0, h].astype(F32)
        S[1, pl.ds(row, W), 0:C] = cache_ref[1, h].astype(F32)
        S[2, pl.ds(row, W), 0:C] = lat_ref[h].astype(F32)
        S[3, pl.ds(row, W), 0:C] = gout_ref[h].astype(F32)

    for n in range(4):
        colsend[0, n, 0:H] = S[n, pl.ds(BASE, H, stride=PITCH)].astype(BF16)
        colsend[1, n, 0:H] = S[n, pl.ds(BASE + W - 1, H, stride=PITCH)].astype(BF16)
        for k, (r, c) in enumerate(((0, 0), (0, W - 1), (H - 1, 0), (H - 1, W - 1))):
            at = BASE + r * PITCH + c
            cornsend[k, n : n + 1] = S[n, at : at + 1]

    pl.semaphore_wait(barrier, len(partners))

    halo = []
    for k, (r, dev) in enumerate(((H - 1, (down, b)), (0, (up, b)))):
        for m, (src, dst) in enumerate(
            (
                (cache_ref.at[:, r], rowbuf.at[k, pl.ds(0, 2)]),
                (lat_ref.at[r], rowbuf.at[k, 2]),
                (gout_ref.at[r], rowbuf.at[k, 3]),
            )
        ):
            halo.append(remote(src, dst, row_s.at[k, m], row_r.at[k, m], dev))
    for k, dev in enumerate(((a, left), (a, right))):
        halo.append(remote(colsend.at[k], colbuf.at[k], col_s.at[k], col_r.at[k], dev))
    for k, dev in enumerate(((up, left), (up, right), (down, left), (down, right))):
        halo.append(remote(cornsend.at[k], cornbuf.at[k], corn_s.at[k], corn_r.at[k], dev))
    for copy in halo:
        copy.start()
    wpieces = [
        remote(Wown, Wp.at[b], wp_s.at[d - 1], wp_r.at[d - 1], (a, (b + d) % 16))
        for d in range(1, 16)
    ]
    for copy in wpieces:
        copy.start()
    Wp[b] = Wown[...]

    row_id = lax.broadcasted_iota(jnp.int32, (128, 128), 0)
    col_id = lax.broadcasted_iota(jnp.int32, (128, 128), 1)
    spread = (row_id % 8 < 6) & (col_id == (row_id // 8) * 6 + row_id % 8)
    spread = jnp.where(spread, 1.0, 0.0).astype(BF16)
    GT[...] = nt(spread, S[3, BASE : BASE + PIX].astype(BF16)).astype(BF16)

    for copy in wpieces:
        copy.wait_recv()
    lane = lax.broadcasted_iota(jnp.int32, (8, 256), 1)
    for tap in range(27):
        total = jnp.zeros((8, 256), F32)
        for j in range(16):
            shift = KB * j - C * tap
            lo, hi = max(0, shift), min(C, shift + KB)
            if lo < hi:
                moved = pltpu.roll(Wp[j].astype(F32), shift % 256, 1)
                total += jnp.where((lane >= lo) & (lane < hi), moved, 0.0)
        for s in slot_of(tap):
            Wl[:, s * 128 : (s + 1) * 128] = total[:, 0:128].astype(BF16)
    mine = pl.ds(pl.multiple_of(core * HALF, 128), HALF)
    peers = [((y + dy) % 4 * 4 + (x + dx) % 4, b) for dy, dx in XY]
    partner = (a, z * 2 + 1 - core)
    wsends = [
        remote(Wl.at[:, mine], Wg.at[a, :, mine], wg_s.at[k], wg_r.at[k], p)
        for k, p in enumerate(peers)
    ]
    for copy in wsends:
        copy.start()
    Wg[a, :, mine] = Wl[:, mine]

    for copy in halo:
        copy.wait_recv()
    for n in range(4):
        S[n, LEAD : LEAD + W, 0:C] = jnp.where(a > 0, rowbuf[0, n].astype(F32), 0.0)
        S[n, BASE + PIX : BASE + PIX + W, 0:C] = jnp.where(a < 15, rowbuf[1, n].astype(F32), 0.0)
        S[n, pl.ds(BASE + W, H, stride=PITCH)] = jnp.where(
            b < 15, colbuf[0, n, 0:H].astype(F32), 0.0
        )
        S[n, pl.ds(BASE - 1, H, stride=PITCH)] = jnp.where(
            b > 0, colbuf[1, n, 0:H].astype(F32), 0.0
        )
        for k, (at, there) in enumerate(
            (
                (BASE + PIX + W, (a < 15) & (b < 15)),
                (BASE + PIX - 1, (a < 15) & (b > 0)),
                (LEAD + W, (a > 0) & (b < 15)),
                (LEAD - 1, (a > 0) & (b > 0)),
            )
        ):
            S[n, at : at + 1] = jnp.where(there, cornbuf[k, n : n + 1], 0.0)

    gain = gpad[...]

    @pl.loop(0, SROWS // 176)
    def _(i):
        rows = pl.ds(pl.multiple_of(i * 176, 8), 176)
        v = S[2, rows]
        scale = lax.rsqrt(jnp.sum(v * v, axis=1, keepdims=True) * (1.0 / C) + 1e-06)
        n = v * scale * gain
        S[2, rows] = n / (1.0 + jnp.exp(-n))

    for n in range(3):
        for c in range(3):
            k = 3 * c + n
            FS[:, k * 128 : (k + 1) * 128] = S[n, 15 + c : 15 + c + FLAT].astype(BF16)

    pairs = []
    for r in range(3):
        part = nn(GT[...], FS[PITCH * r : PITCH * r + PIX])
        for c in range(3):
            for t in range(3):
                k = 3 * c + t
                block = part[:, k * 128 : (k + 1) * 128].reshape(16, 8, 128)
                for s in slot_of(9 * t + 3 * r + c):
                    Rs[:, :, s * 128 : (s + 1) * 128] = block
        lo, hi = CHUNKS[r]
        pair = remote(
            Rs.at[:, :, tiles(1 - core, lo, hi)],
            RC.at[:, :, lo * 128 : hi * 128],
            rc_s.at[r],
            rc_r.at[r],
            partner,
        )
        pair.start()
        pairs.append(pair)
        if r == 1:
            for copy in wsends:
                copy.wait_recv()
            wswap = remote(Wg.at[:, :, mine], Wg.at[:, :, mine], wc_s, wc_r, partner)
            wswap.start()

    asends = []
    for n, (lo, hi) in enumerate(SUMS):
        lanes = slice(lo * 128, hi * 128)
        if n == 0:
            pairs[0].wait_recv()
            pairs[1].wait_recv()
        else:
            for c in range(3):
                FG[:, c * 128 : (c + 1) * 128] = S[3, 15 + c : 15 + c + FLAT].astype(BF16)
            pairs[2].wait_recv()

        @pl.loop(0, 16)
        def _(k):
            SB[k, :, lanes] = (Rs[k, :, tiles(core, lo, hi)] + RC[k, :, lanes]).astype(BF16)

        for k, p in enumerate(peers):
            copy = remote(
                SB.at[p[0], :, lanes], RA.at[k, :, lanes], ra_s.at[n, k], ra_r.at[n, k], p
            )
            copy.start()
            asends.append(copy)

    wswap.wait()
    compact = (row_id < C) & (col_id == (row_id // 6) * 8 + row_id % 6)
    compact = jnp.where(compact, 1.0, 0.0).astype(BF16)
    for tap in range(27):
        s = slot_of(tap)[0]
        block = Wg[:, :, s * 128 : (s + 1) * 128].astype(F32).reshape(128, 128)
        block = nn(compact, block.astype(BF16)).astype(BF16)
        t, r, c = tap // 9, tap // 3 % 3, tap % 3
        Wn[r, :, (3 * c + t) * 128 : (3 * c + t + 1) * 128] = block
        if t == 2:
            Wb[r, (2 - c) * 128 : (3 - c) * 128] = block

    def rows_step(i):
        h0 = i * ROWS
        at = pl.multiple_of(h0 * PITCH, 16)
        acc = nt(FS[pl.ds(at, ROWS * PITCH)], Wn[0])
        acc += nt(FS[pl.ds(at + PITCH, ROWS * PITCH)], Wn[1])
        acc += nt(FS[pl.ds(at + 2 * PITCH, ROWS * PITCH)], Wn[2])
        acc = acc.reshape(ROWS, PITCH, 128)[:, 0:W, 0:C]
        lat = lat_ref[pl.ds(h0, ROWS)].astype(F32)
        out_ref[pl.ds(h0, ROWS)] = (lat + bias_ref[...].reshape(1, 1, C) + acc).astype(BF16)

        back = nn(FG[pl.ds(at + 2 * PITCH, ROWS * PITCH)], Wb[0])
        back += nn(FG[pl.ds(at + PITCH, ROWS * PITCH)], Wb[1])
        back += nn(FG[pl.ds(at, ROWS * PITCH)], Wb[2])
        dact = back.reshape(ROWS, PITCH, 128)[:, 0:W, 0:C]
        g = gain_ref[...].reshape(1, 1, C)
        scale = lax.rsqrt(jnp.sum(lat * lat, axis=2, keepdims=True) * (1.0 / C) + 1e-06)
        n = lat * scale * g
        sig = 1.0 / (1.0 + jnp.exp(-n))
        du = dact * (sig * (1.0 + n * (1.0 - sig))) * g
        inner = jnp.sum(lat * du, axis=2, keepdims=True) * (1.0 / C)
        dlat = scale * du - lat * (scale * scale * scale * inner)
        glat_ref[pl.ds(h0, ROWS)] = (gout_ref[pl.ds(h0, ROWS)].astype(F32) + dlat).astype(BF16)

    pl.loop(0, EARLY)(rows_step)

    for copy in asends:
        copy.wait_recv()
    total = Rs[a, :, mine] + RC[a]
    for k in range(15):
        total += RA[k].astype(F32)
    T[...] = total
    for half in range(2):

        @pl.when(core == half)
        def _():
            for j in range(8):
                piece = jnp.zeros((8, 256), F32)
                for m in range(14):
                    shift = C * m - (KB * j + 48 * half)
                    lo, hi = max(0, shift), min(KB, shift + C)
                    if lo < hi:
                        s = ORDER[half].index(13 * half + m)
                        block = jnp.concatenate(
                            [T[:, s * 128 : (s + 1) * 128], jnp.zeros((8, 128), F32)], axis=1
                        )
                        moved = pltpu.roll(block, shift % 256, 1)
                        piece += jnp.where((lane >= lo) & (lane < hi), moved, 0.0)
                PZ[j] = piece

    zsends = []
    for j in range(8):
        oz, oc = 4 * core + j // 2, j % 2
        itself = (oz == z) & (oc == core)
        copy = remote(PZ.at[j], RZ.at[z], rz_s.at[j], rz_r.at[z], (a, oz * 2 + oc))
        zsends.append((itself, copy))

        @pl.when(jnp.logical_not(itself))
        def _():
            copy.start()

        @pl.when(itself)
        def _():
            RZ[z] = PZ[j]

    pl.loop(EARLY, H // ROWS)(rows_step)

    for k in range(8):
        source = (a, k * 2 + z // 4)

        @pl.when(jnp.logical_not((k == z) & (z // 4 == core)))
        def _():
            remote(PZ.at[0], RZ.at[k], rz_s.at[0], rz_r.at[k], source).wait_recv()

    final = RZ[0]
    for k in range(1, 8):
        final += RZ[k]
    gw_ref[...] = final[0:6, 0:KB]

    for copy in halo + wpieces + wsends + pairs + asends:
        copy.wait_send()
    for itself, copy in zsends:

        @pl.when(jnp.logical_not(itself))
        def _():
            copy.wait_send()


def local(latent, frame_cache, norm_gain, conv_bias, conv_weight, grad_out):
    vmem = pl.BlockSpec(memory_space=pltpu.VMEM)
    dma = pltpu.SemaphoreType.DMA
    return pl.pallas_call(
        kernel,
        out_shape=(
            jax.ShapeDtypeStruct((H, W, C), BF16),
            jax.ShapeDtypeStruct((H, W, C), BF16),
            jax.ShapeDtypeStruct((6, KB), F32),
        ),
        in_specs=[vmem] * 6,
        out_specs=(vmem, vmem, vmem),
        scratch_shapes=[
            pltpu.VMEM((4, SROWS, 128), F32),
            pltpu.VMEM((FLAT, 9 * 128), BF16),
            pltpu.VMEM((FLAT, 3 * 128), BF16),
            pltpu.VMEM((128, PIX), BF16),
            pltpu.VMEM((1, 128), F32),
            pltpu.VMEM((2, 4, W, C), BF16),
            pltpu.VMEM((2, 4, 48, 128), BF16),
            pltpu.VMEM((2, 4, 48, 128), BF16),
            pltpu.VMEM((4, 8, 128), F32),
            pltpu.VMEM((4, 8, 128), F32),
            pltpu.VMEM((8, 256), F32),
            pltpu.VMEM((8, 256), BF16),
            pltpu.VMEM((16, 8, 256), BF16),
            pltpu.VMEM((8, 2 * HALF), BF16),
            pltpu.VMEM((16, 8, 2 * HALF), BF16),
            pltpu.VMEM((3, 128, 9 * 128), BF16),
            pltpu.VMEM((3, 3 * 128, 128), BF16),
            pltpu.VMEM((16, 8, 2 * HALF), F32),
            pltpu.VMEM((16, 8, HALF), F32),
            pltpu.VMEM((16, 8, HALF), BF16),
            pltpu.VMEM((15, 8, HALF), BF16),
            pltpu.VMEM((8, HALF), F32),
            pltpu.VMEM((8, 8, 256), F32),
            pltpu.VMEM((8, 8, 256), F32),
            dma((2, 3)), dma((2, 3)), dma((2,)), dma((2,)), dma((4,)), dma((4,)),
            dma((15,)), dma((15,)), dma((15,)), dma((15,)), dma, dma,
            dma((3,)), dma((3,)), dma((2, 15)), dma((2, 15)), dma((8,)), dma((8,)),
        ],
        compiler_params=pltpu.CompilerParams(
            collective_id=0, has_side_effects=True, vmem_limit_bytes=60 * 1024 * 1024
        ),
    )(
        latent, frame_cache, norm_gain.reshape(1, C), conv_bias.reshape(1, C), conv_weight, grad_out
    )


def solution(mesh):
    placed = (
        P("ha", "wa", None),
        P(None, "ha", "wa", None),
        P(),
        P(),
        P("ha", "wa"),
        P("ha", "wa", None),
    )
    return jax.shard_map(
        local,
        mesh=mesh,
        in_specs=placed,
        out_specs=(P("ha", "wa", None), P("ha", "wa", None), P("ha", "wa")),
        check_vma=False,
    )
```

```python
import jax
import jax.numpy as jnp
from jax import lax
from jax.experimental import pallas as pl
from jax.experimental.pallas import tpu as pltpu
from jax.sharding import PartitionSpec as P

MESH = pl.DeviceIdType.MESH
F32 = jnp.float32
BF16 = jnp.bfloat16

H = 45
W = 40
C = 96
PITCH = 48
LEAD = 16
FLAT = (H + 2) * PITCH
PIX = H * PITCH
SROWS = LEAD + FLAT + 16
BASE = LEAD + PITCH
KB = 162
HALF = 14 * 128
ROWS = 9
EARLY = 3
XY = [(dy, dx) for dy in range(4) for dx in range(4) if (dy, dx) != (0, 0)]
XY.sort(key=lambda p: -(min(p[0], 4 - p[0]) + min(p[1], 4 - p[1])))


ORDER = (
    (0, 1, 2, 9, 10, 11, 3, 4, 5, 12, 13, 6, 7, 8),
    (18, 19, 20, 13, 14, 21, 22, 23, 15, 16, 17, 24, 25, 26),
)
CHUNKS = ((0, 3), (3, 8), (8, 14))
SUMS = ((0, 8), (8, 14))


def slot_of(tap):
    return [14 * half + ORDER[half].index(tap) for half in (0, 1) if tap in ORDER[half]]


def tiles(core, lo, hi):
    return pl.ds(pl.multiple_of(core * HALF + lo * 128, 128), (hi - lo) * 128)


def nt(a, b):
    return lax.dot_general(a, b, (((1,), (1,)), ((), ())), preferred_element_type=F32)


def nn(a, b):
    return lax.dot_general(a, b, (((1,), (0,)), ((), ())), preferred_element_type=F32)


def remote(src, dst, send, recv, device):
    return pltpu.make_async_remote_copy(
        src_ref=src, dst_ref=dst, send_sem=send, recv_sem=recv, device_id=device, device_id_type=MESH
    )


def kernel(
    lat_ref, cache_ref, gain_ref, bias_ref, w_ref, gout_ref,
    out_ref, glat_ref, gw_ref,
    S, FS, FG, GT, gpad,
    rowbuf, colsend, colbuf, cornsend, cornbuf,
    Wtmp, Wown, Wp, Wl, Wg, Wn, Wb,
    Rs, RC, SB, RA, T, PZ, RZ,
    row_s, row_r, col_s, col_r, corn_s, corn_r,
    wp_s, wp_r, wg_s, wg_r, wc_s, wc_r,
    rc_s, rc_r, ra_s, ra_r, rz_s, rz_r, obuf, gbuf, res_s,
):
    a = lax.axis_index("ha")
    b = lax.axis_index("wa")
    y, x = a // 4, a % 4
    z, core = b // 2, b % 2
    up, down = (a + 15) % 16, (a + 1) % 16
    left, right = (b + 15) % 16, (b + 1) % 16

    barrier = pltpu.get_barrier_semaphore()
    partners = [(a, (b + d) % 16) for d in range(1, 16)]
    partners += [((a + d) % 16, b) for d in range(1, 16)]
    partners += [(v, h) for v in (up, down) for h in (left, right)]
    for p in partners:
        pl.semaphore_signal(barrier, inc=1, device_id=p, device_id_type=MESH)

    S[...] = jnp.zeros_like(S)
    gpad[...] = jnp.zeros_like(gpad)
    gpad[:, 0:C] = gain_ref[...]
    Wtmp[...] = jnp.zeros_like(Wtmp)
    Wtmp[0:6, 0:KB] = w_ref[...].astype(F32)
    Wown[...] = Wtmp[...].astype(BF16)

    @pl.loop(0, H)
    def _(h):
        row = pl.multiple_of(BASE + h * PITCH, 8)
        S[0, pl.ds(row, W), 0:C] = cache_ref[0, h].astype(F32)
        S[1, pl.ds(row, W), 0:C] = cache_ref[1, h].astype(F32)
        S[2, pl.ds(row, W), 0:C] = lat_ref[h].astype(F32)
        S[3, pl.ds(row, W), 0:C] = gout_ref[h].astype(F32)

    for n in range(4):
        colsend[0, n, 0:H] = S[n, pl.ds(BASE, H, stride=PITCH)].astype(BF16)
        colsend[1, n, 0:H] = S[n, pl.ds(BASE + W - 1, H, stride=PITCH)].astype(BF16)
        for k, (r, c) in enumerate(((0, 0), (0, W - 1), (H - 1, 0), (H - 1, W - 1))):
            at = BASE + r * PITCH + c
            cornsend[k, n : n + 1] = S[n, at : at + 1]

    pl.semaphore_wait(barrier, len(partners))

    halo = []
    for k, (r, dev) in enumerate(((H - 1, (down, b)), (0, (up, b)))):
        for m, (src, dst) in enumerate(
            (
                (cache_ref.at[:, r], rowbuf.at[k, pl.ds(0, 2)]),
                (lat_ref.at[r], rowbuf.at[k, 2]),
                (gout_ref.at[r], rowbuf.at[k, 3]),
            )
        ):
            halo.append(remote(src, dst, row_s.at[k, m], row_r.at[k, m], dev))
    for k, dev in enumerate(((a, left), (a, right))):
        halo.append(remote(colsend.at[k], colbuf.at[k], col_s.at[k], col_r.at[k], dev))
    for k, dev in enumerate(((up, left), (up, right), (down, left), (down, right))):
        halo.append(remote(cornsend.at[k], cornbuf.at[k], corn_s.at[k], corn_r.at[k], dev))
    for copy in halo:
        copy.start()
    wpieces = [
        remote(Wown, Wp.at[b], wp_s.at[d - 1], wp_r.at[d - 1], (a, (b + d) % 16))
        for d in range(1, 16)
    ]
    for copy in wpieces:
        copy.start()
    Wp[b] = Wown[...]

    row_id = lax.broadcasted_iota(jnp.int32, (128, 128), 0)
    col_id = lax.broadcasted_iota(jnp.int32, (128, 128), 1)
    spread = (row_id % 8 < 6) & (col_id == (row_id // 8) * 6 + row_id % 8)
    spread = jnp.where(spread, 1.0, 0.0).astype(BF16)
    GT[...] = nt(spread, S[3, BASE : BASE + PIX].astype(BF16)).astype(BF16)

    for copy in wpieces:
        copy.wait_recv()
    lane = lax.broadcasted_iota(jnp.int32, (8, 256), 1)
    for tap in range(27):
        total = jnp.zeros((8, 256), F32)
        for j in range(16):
            shift = KB * j - C * tap
            lo, hi = max(0, shift), min(C, shift + KB)
            if lo < hi:
                moved = pltpu.roll(Wp[j].astype(F32), shift % 256, 1)
                total += jnp.where((lane >= lo) & (lane < hi), moved, 0.0)
        for s in slot_of(tap):
            Wl[:, s * 128 : (s + 1) * 128] = total[:, 0:128].astype(BF16)
    mine = pl.ds(pl.multiple_of(core * HALF, 128), HALF)
    peers = [((y + dy) % 4 * 4 + (x + dx) % 4, b) for dy, dx in XY]
    partner = (a, z * 2 + 1 - core)
    wsends = [
        remote(Wl.at[:, mine], Wg.at[a, :, mine], wg_s.at[k], wg_r.at[k], p)
        for k, p in enumerate(peers)
    ]
    for copy in wsends:
        copy.start()
    Wg[a, :, mine] = Wl[:, mine]

    for copy in halo:
        copy.wait_recv()
    for n in range(4):
        S[n, LEAD : LEAD + W, 0:C] = jnp.where(a > 0, rowbuf[0, n].astype(F32), 0.0)
        S[n, BASE + PIX : BASE + PIX + W, 0:C] = jnp.where(a < 15, rowbuf[1, n].astype(F32), 0.0)
        S[n, pl.ds(BASE + W, H, stride=PITCH)] = jnp.where(
            b < 15, colbuf[0, n, 0:H].astype(F32), 0.0
        )
        S[n, pl.ds(BASE - 1, H, stride=PITCH)] = jnp.where(
            b > 0, colbuf[1, n, 0:H].astype(F32), 0.0
        )
        for k, (at, there) in enumerate(
            (
                (BASE + PIX + W, (a < 15) & (b < 15)),
                (BASE + PIX - 1, (a < 15) & (b > 0)),
                (LEAD + W, (a > 0) & (b < 15)),
                (LEAD - 1, (a > 0) & (b > 0)),
            )
        ):
            S[n, at : at + 1] = jnp.where(there, cornbuf[k, n : n + 1], 0.0)

    gain = gpad[...]

    @pl.loop(0, SROWS // 176)
    def _(i):
        rows = pl.ds(pl.multiple_of(i * 176, 8), 176)
        v = S[2, rows]
        scale = lax.rsqrt(jnp.sum(v * v, axis=1, keepdims=True) * (1.0 / C) + 1e-06)
        n = v * scale * gain
        S[2, rows] = n / (1.0 + jnp.exp(-n))

    for n in range(3):
        for c in range(3):
            k = 3 * c + n
            FS[:, k * 128 : (k + 1) * 128] = S[n, 15 + c : 15 + c + FLAT].astype(BF16)

    pairs = []
    for r in range(3):
        part = nn(GT[...], FS[PITCH * r : PITCH * r + PIX])
        for c in range(3):
            for t in range(3):
                k = 3 * c + t
                block = part[:, k * 128 : (k + 1) * 128].reshape(16, 8, 128)
                for s in slot_of(9 * t + 3 * r + c):
                    Rs[:, :, s * 128 : (s + 1) * 128] = block
        lo, hi = CHUNKS[r]
        pair = remote(
            Rs.at[:, :, tiles(1 - core, lo, hi)],
            RC.at[:, :, lo * 128 : hi * 128],
            rc_s.at[r],
            rc_r.at[r],
            partner,
        )
        pair.start()
        pairs.append(pair)
        if r == 1:
            for copy in wsends:
                copy.wait_recv()
            wswap = remote(Wg.at[:, :, mine], Wg.at[:, :, mine], wc_s, wc_r, partner)
            wswap.start()

    asends = []
    for n, (lo, hi) in enumerate(SUMS):
        lanes = slice(lo * 128, hi * 128)
        if n == 0:
            pairs[0].wait_recv()
            pairs[1].wait_recv()
        else:
            for c in range(3):
                FG[:, c * 128 : (c + 1) * 128] = S[3, 15 + c : 15 + c + FLAT].astype(BF16)
            pairs[2].wait_recv()

        @pl.loop(0, 16)
        def _(k):
            SB[k, :, lanes] = (Rs[k, :, tiles(core, lo, hi)] + RC[k, :, lanes]).astype(BF16)

        for k, p in enumerate(peers):
            copy = remote(
                SB.at[p[0], :, lanes], RA.at[k, :, lanes], ra_s.at[n, k], ra_r.at[n, k], p
            )
            copy.start()
            asends.append(copy)

    wswap.wait()
    compact = (row_id < C) & (col_id == (row_id // 6) * 8 + row_id % 6)
    compact = jnp.where(compact, 1.0, 0.0).astype(BF16)
    for tap in range(27):
        s = slot_of(tap)[0]
        block = Wg[:, :, s * 128 : (s + 1) * 128].astype(F32).reshape(128, 128)
        block = nn(compact, block.astype(BF16)).astype(BF16)
        t, r, c = tap // 9, tap // 3 % 3, tap % 3
        Wn[r, :, (3 * c + t) * 128 : (3 * c + t + 1) * 128] = block
        if t == 2:
            Wb[r, (2 - c) * 128 : (3 - c) * 128] = block

    def results(h0):
        rows = pl.ds(h0, ROWS)
        return (
            pltpu.make_async_copy(obuf.at[rows], out_ref.at[rows], res_s.at[0]),
            pltpu.make_async_copy(gbuf.at[rows], glat_ref.at[rows], res_s.at[1]),
        )

    def rows_step(i):
        h0 = i * ROWS
        at = pl.multiple_of(h0 * PITCH, 16)
        acc = nt(FS[pl.ds(at, ROWS * PITCH)], Wn[0])
        acc += nt(FS[pl.ds(at + PITCH, ROWS * PITCH)], Wn[1])
        acc += nt(FS[pl.ds(at + 2 * PITCH, ROWS * PITCH)], Wn[2])
        acc = acc.reshape(ROWS, PITCH, 128)[:, 0:W, 0:C]
        lat = lat_ref[pl.ds(h0, ROWS)].astype(F32)
        obuf[pl.ds(h0, ROWS)] = (lat + bias_ref[...].reshape(1, 1, C) + acc).astype(BF16)

        back = nn(FG[pl.ds(at + 2 * PITCH, ROWS * PITCH)], Wb[0])
        back += nn(FG[pl.ds(at + PITCH, ROWS * PITCH)], Wb[1])
        back += nn(FG[pl.ds(at, ROWS * PITCH)], Wb[2])
        dact = back.reshape(ROWS, PITCH, 128)[:, 0:W, 0:C]
        g = gain_ref[...].reshape(1, 1, C)
        scale = lax.rsqrt(jnp.sum(lat * lat, axis=2, keepdims=True) * (1.0 / C) + 1e-06)
        n = lat * scale * g
        sig = 1.0 / (1.0 + jnp.exp(-n))
        du = dact * (sig * (1.0 + n * (1.0 - sig))) * g
        inner = jnp.sum(lat * du, axis=2, keepdims=True) * (1.0 / C)
        dlat = scale * du - lat * (scale * scale * scale * inner)
        gbuf[pl.ds(h0, ROWS)] = (gout_ref[pl.ds(h0, ROWS)].astype(F32) + dlat).astype(BF16)
        for copy in results(h0):
            copy.start()

    pl.loop(0, EARLY)(rows_step)

    for copy in asends:
        copy.wait_recv()
    total = Rs[a, :, mine] + RC[a]
    for k in range(15):
        total += RA[k].astype(F32)
    T[...] = total
    for half in range(2):

        @pl.when(core == half)
        def _():
            for j in range(8):
                piece = jnp.zeros((8, 256), F32)
                for m in range(14):
                    shift = C * m - (KB * j + 48 * half)
                    lo, hi = max(0, shift), min(KB, shift + C)
                    if lo < hi:
                        s = ORDER[half].index(13 * half + m)
                        block = jnp.concatenate(
                            [T[:, s * 128 : (s + 1) * 128], jnp.zeros((8, 128), F32)], axis=1
                        )
                        moved = pltpu.roll(block, shift % 256, 1)
                        piece += jnp.where((lane >= lo) & (lane < hi), moved, 0.0)
                PZ[j] = piece

    zsends = []
    for j in range(8):
        oz, oc = 4 * core + j // 2, j % 2
        itself = (oz == z) & (oc == core)
        copy = remote(PZ.at[j], RZ.at[z], rz_s.at[j], rz_r.at[z], (a, oz * 2 + oc))
        zsends.append((itself, copy))

        @pl.when(jnp.logical_not(itself))
        def _():
            copy.start()

        @pl.when(itself)
        def _():
            RZ[z] = PZ[j]

    pl.loop(EARLY, H // ROWS)(rows_step)

    for k in range(8):
        source = (a, k * 2 + z // 4)

        @pl.when(jnp.logical_not((k == z) & (z // 4 == core)))
        def _():
            remote(PZ.at[0], RZ.at[k], rz_s.at[0], rz_r.at[k], source).wait_recv()

    final = RZ[0]
    for k in range(1, 8):
        final += RZ[k]
    gw_ref[...] = final[0:6, 0:KB]

    for i in range(H // ROWS):
        for copy in results(i * ROWS):
            copy.wait()
    for copy in halo + wpieces + wsends + pairs + asends:
        copy.wait_send()
    for itself, copy in zsends:

        @pl.when(jnp.logical_not(itself))
        def _():
            copy.wait_send()


def local(latent, frame_cache, norm_gain, conv_bias, conv_weight, grad_out):
    vmem = pl.BlockSpec(memory_space=pltpu.VMEM)
    any_ = pl.BlockSpec(memory_space=pl.ANY)
    dma = pltpu.SemaphoreType.DMA
    return pl.pallas_call(
        kernel,
        out_shape=(
            jax.ShapeDtypeStruct((H, W, C), BF16),
            jax.ShapeDtypeStruct((H, W, C), BF16),
            jax.ShapeDtypeStruct((6, KB), F32),
        ),
        in_specs=[vmem] * 6,
        out_specs=(any_, any_, vmem),
        scratch_shapes=[
            pltpu.VMEM((4, SROWS, 128), F32),
            pltpu.VMEM((FLAT, 9 * 128), BF16),
            pltpu.VMEM((FLAT, 3 * 128), BF16),
            pltpu.VMEM((128, PIX), BF16),
            pltpu.VMEM((1, 128), F32),
            pltpu.VMEM((2, 4, W, C), BF16),
            pltpu.VMEM((2, 4, 48, 128), BF16),
            pltpu.VMEM((2, 4, 48, 128), BF16),
            pltpu.VMEM((4, 8, 128), F32),
            pltpu.VMEM((4, 8, 128), F32),
            pltpu.VMEM((8, 256), F32),
            pltpu.VMEM((8, 256), BF16),
            pltpu.VMEM((16, 8, 256), BF16),
            pltpu.VMEM((8, 2 * HALF), BF16),
            pltpu.VMEM((16, 8, 2 * HALF), BF16),
            pltpu.VMEM((3, 128, 9 * 128), BF16),
            pltpu.VMEM((3, 3 * 128, 128), BF16),
            pltpu.VMEM((16, 8, 2 * HALF), F32),
            pltpu.VMEM((16, 8, HALF), F32),
            pltpu.VMEM((16, 8, HALF), BF16),
            pltpu.VMEM((15, 8, HALF), BF16),
            pltpu.VMEM((8, HALF), F32),
            pltpu.VMEM((8, 8, 256), F32),
            pltpu.VMEM((8, 8, 256), F32),
            dma((2, 3)), dma((2, 3)), dma((2,)), dma((2,)), dma((4,)), dma((4,)),
            dma((15,)), dma((15,)), dma((15,)), dma((15,)), dma, dma,
            dma((3,)), dma((3,)), dma((2, 15)), dma((2, 15)), dma((8,)), dma((8,)),
            pltpu.VMEM((H, W, C), BF16), pltpu.VMEM((H, W, C), BF16), dma((2,)),
        ],
        compiler_params=pltpu.CompilerParams(
            collective_id=0, has_side_effects=True, vmem_limit_bytes=60 * 1024 * 1024
        ),
    )(
        latent, frame_cache, norm_gain.reshape(1, C), conv_bias.reshape(1, C), conv_weight, grad_out
    )


def solution(mesh):
    placed = (
        P("ha", "wa", None),
        P(None, "ha", "wa", None),
        P(),
        P(),
        P("ha", "wa"),
        P("ha", "wa", None),
    )
    return jax.shard_map(
        local,
        mesh=mesh,
        in_specs=placed,
        out_specs=(P("ha", "wa", None), P("ha", "wa", None), P("ha", "wa")),
        check_vma=False,
    )
```
